32 devices in a mesh: group: 2 (over y), ctx: 8 (over z, x), tp: 2 (over core).
Axes of the slice: x: 2, y: 2, z: 4, core: 2. Of those that a mesh axis runs over, the one named last changes fastest.
Arguments:
- queries: bfloat16 [2048, 4096], P(('group', 'ctx'), 'tp'), parts along dimension 0, may hold values from -1.796875 to 1.796875
- key_rows: bfloat16 [2048, 4096], P(('group', 'ctx'), 'tp'), parts along dimension 0, may hold values from -1.796875 to 1.796875
- value_rows: bfloat16 [2048, 4096], P(('group', 'ctx'), 'tp'), parts along dimension 0, may hold values from -6 to 6
- out_grad: bfloat16 [2048, 4096], P(('group', 'ctx', 'tp')), parts along dimension 0, may hold values from -0.119628906 to 0.119628906
- log_decay: float32 [2048, 32], P(('group', 'ctx'), 'tp'), parts along dimension 0, may hold values from -0.8 to 0
- doc_ids: int32 [32], P('group'), parts along dimension 0, may hold values from 0 to 3, never falling along the last dimension, each value on 1 to 8 neighbouring positions
Outputs:
- key_grad: bfloat16 [2048, 4096], P(('group', 'ctx'), 'tp'), parts along dimension 0
- value_grad: bfloat16 [2048, 4096], P(('group', 'ctx'), 'tp'), parts along dimension 0
The draws below stay inside these ranges and needn't reach their ends.
There are 2 independent parts, one for each index of `group`. The reference program is written for one: setup_inputs(seed, part) draws one part's arguments, and reference() takes and returns one part's arrays. A program takes and returns all parts, laid end to end along the dimension named above; each array names one. Nothing has to cross between parts.
Inputs may be any that keep to these rules, and one draw needn't show every extreme that they name: `doc_ids`: one entry per block of 64 positions; each document covers 1 to 8 consecutive blocks, one exactly 8; document numbers never fall.
All inputs are finite; a program needn't handle non-finite values.
Results may differ from the reference program's by a relative error of at most 0.0056.
Values may be sent and summed in bfloat16 or wider, within the bound.
A program may use at most 64 MiB of HBM per device.

```python
import math
import jax
import jax.numpy as jnp
import numpy as np
from jax import lax

H = 32
DH = 128
BLOCK = 64
DOCS = 4
ROWS = 128
SEQ = 1024
BLOCKS = 16


def draw_log_decay(key, part):
    streams = jax.random.split(jax.random.fold_in(key, 17), 6)
    fast_share = 0.5
    head_fast = jax.random.uniform(streams[0], (H,)) < fast_share
    fast_rate = jax.random.uniform(streams[1], (H,), minval=1.0 / 50.0, maxval=1.0 / 30.0)
    slow_rate = jax.random.uniform(streams[2], (H,), minval=0.1, maxval=0.8) / SEQ
    base_rate = jnp.where(head_fast, fast_rate, slow_rate)
    roughness = jnp.exp(jax.random.uniform(streams[3], (SEQ, H), minval=-0.69, maxval=0.69))
    bursting = jax.random.uniform(streams[4], (SEQ, H)) < 3.0 / SEQ
    dropped = jnp.log(jax.random.uniform(streams[5], (SEQ, H), minval=0.5, maxval=0.8))
    values_out = -base_rate[None, :] * roughness + jnp.where(bursting, dropped, 0.0)
    return values_out.astype(jnp.float32)


def level_of(own_key, extent, shards, least, top_value):
    gain = 1.0
    for dim, shards_of in shards:
        steps = jax.random.uniform(jax.random.fold_in(jax.random.fold_in(own_key, 6), dim), (shards_of,), jnp.float32, least / len(shards), top_value / len(shards))
        gain = gain * jnp.repeat(jnp.exp(steps), extent[dim] // shards_of).reshape((-1,) + (1,) * (len(extent) - 1 - dim))
    return gain


def split_up(number_of, total, limit, lean):
    weights = [(1 << 20) // math.isqrt(standing ** lean) + 1 for standing in range(2, number_of + 1)]
    rest, counts = total - limit - (number_of - 1), [1] * (number_of - 1)
    while rest > 0:
        candidates = [i for i in range(number_of - 1) if counts[i] < limit]
        pool, left = sum([weights[i] for i in candidates]), rest
        for i in candidates:
            extra = min(limit - counts[i], max(1, left * weights[i] // pool), rest)
            counts[i] = counts[i] + extra
            rest = rest - extra
    return np.array([limit] + counts)


def ragged(stream_key, count, total, limit, lean):
    if count == 2:
        one = jax.random.randint(stream_key, (), max(1, total - limit), min(limit, total - 1) + 1)
        return jnp.stack([one, total - one])
    tallies = jnp.asarray(split_up(count, total, limit, lean), jnp.int32)
    couples = (count - 1) // 2
    donor, taker = tallies[1:1 + 2 * couples:2], tallies[2:2 + 2 * couples:2]
    room = jnp.minimum(donor - 1, limit - taker)
    shifted = jax.random.randint(jax.random.fold_in(stream_key, 1), (couples,), 0, 1 << 20) % (room + 1)
    tallies = tallies.at[1:1 + 2 * couples:2].set(donor - shifted).at[2:2 + 2 * couples:2].set(taker + shifted)
    return tallies[jax.random.permutation(jax.random.fold_in(stream_key, 2), count)]


def scatter_about(stream_key, shape, deviation, reach, cuts=(), kind=jnp.bfloat16):
    result = deviation * jax.random.normal(stream_key, shape, jnp.float32)
    if cuts:
        result = result * level_of(stream_key, shape, cuts, -0.22, 0.18)
    return jnp.clip(result, -reach, reach).astype(kind)


def setup_inputs(seed: int = 0, part: int = 0) -> dict:
    keys = jax.random.split(jax.random.key(seed), 7)
    part_splits = jax.random.split(jax.random.fold_in(keys[6], part), 7)
    queries = scatter_about(part_splits[0], (SEQ, H * DH), 0.3, 1.796875, ((0, 8), (1, 2)))
    key_rows = scatter_about(part_splits[1], (SEQ, H * DH), 0.3, 1.796875, ((0, 8), (1, 2)))
    value_rows = scatter_about(part_splits[2], (SEQ, H * DH), 1.0, 6.0, ((0, 8), (1, 2)))
    out_grad = scatter_about(part_splits[3], (SEQ, H * DH), 0.02, 0.119628906, ((0, 16),))
    log_decay = draw_log_decay(jax.random.fold_in(jax.random.fold_in(keys[6], part), 71), part)
    doc_ids = jnp.searchsorted(jnp.cumsum(ragged(part_splits[5], DOCS, BLOCKS, BLOCKS // 2, 0)), jnp.arange(BLOCKS), side="right").astype(jnp.int32)
    return dict(queries=queries, key_rows=key_rows, value_rows=value_rows, out_grad=out_grad, log_decay=log_decay, doc_ids=doc_ids)


def product(pattern, first_op, second_op, promote):
    if promote:
        first_op = lax.optimization_barrier(first_op)
        second_op = lax.optimization_barrier(second_op)
        return jnp.einsum(pattern, first_op.astype(jnp.float32), second_op.astype(jnp.float32))
    return jnp.einsum(pattern, first_op, second_op, preferred_element_type=jnp.float32)


def span_terms(queries, key_rows, value_rows, grad_rows, log_decay, doc_rows, prev_doc, promote):
    row_count, head_count = log_decay.shape
    head_size = queries.shape[1] // head_count
    query_heads = queries.reshape(row_count, head_count, head_size)
    key_heads = key_rows.reshape(row_count, head_count, head_size)
    value_heads = value_rows.reshape(row_count, head_count, head_size)
    grad_heads = grad_rows.reshape(row_count, head_count, head_size)
    cumulative = jnp.cumsum(log_decay.T.astype(jnp.float32), axis=1)
    spread = cumulative[:, :, None] - cumulative[:, None, :]
    position = jnp.arange(row_count)
    allowed = (position[:, None] >= position[None, :]) & (doc_rows[:, None] == doc_rows[None, :])
    weight = jnp.where(allowed[None], jnp.exp(jnp.minimum(spread, 0.0)), 0.0)
    grad_value = product("thd,shd->hts", grad_heads, value_heads, promote)
    query_key = product("thd,shd->hts", query_heads, key_heads, promote)
    mixed_gv = (weight * grad_value).astype(jnp.bfloat16)
    mixed_qk = (weight * query_key).astype(jnp.bfloat16)
    key_inner = product("hts,thd->shd", mixed_gv, query_heads, promote)
    value_inner = product("hts,thd->shd", mixed_qk, grad_heads, promote)
    first_doc = doc_rows[0]
    last_doc = doc_rows[-1]
    linked = (prev_doc == first_doc).astype(jnp.float32)
    lead_mask = (doc_rows == first_doc).astype(jnp.float32)
    scaling = jnp.exp(cumulative).T * lead_mask[:, None]
    scaled = (query_heads.astype(jnp.float32) * scaling[:, :, None]).astype(jnp.bfloat16)
    state = product("thi,thj->hij", scaled, grad_heads, promote) * linked
    through = linked * (first_doc == last_doc).astype(jnp.float32)
    factor = through * jnp.exp(cumulative[:, -1])
    tail_mask = (doc_rows == last_doc).astype(jnp.float32)
    weight_in = jnp.exp(cumulative[:, -1:] - cumulative) * tail_mask[None, :]
    return key_inner, value_inner, state, factor, weight_in


def apply_state(incoming, key_rows, value_rows, weight_in, key_inner, value_inner, promote):
    row_count = key_rows.shape[0]
    head_count, head_size = incoming.shape[0], incoming.shape[1]
    key_heads = key_rows.reshape(row_count, head_count, head_size)
    value_heads = value_rows.reshape(row_count, head_count, head_size)
    rounded = incoming.astype(jnp.bfloat16)
    to_keys = product("hij,shj->shi", rounded, value_heads, promote)
    to_values = product("hij,shi->shj", rounded, key_heads, promote)
    scaling = weight_in.T[:, :, None]
    key_grad = (key_inner + scaling * to_keys).astype(jnp.bfloat16).reshape(row_count, head_count * head_size)
    value_grad = (value_inner + scaling * to_values).astype(jnp.bfloat16).reshape(row_count, head_count * head_size)
    return key_grad, value_grad


def reference(queries, key_rows, value_rows, out_grad, log_decay, doc_ids):
    span_count = SEQ // ROWS
    feature_count = H * DH
    query_spans = queries.reshape(span_count, ROWS, feature_count)
    key_spans = key_rows.reshape(span_count, ROWS, feature_count)
    value_spans = value_rows.reshape(span_count, ROWS, feature_count)
    grad_spans = out_grad.reshape(span_count, ROWS, feature_count)
    decay_spans = log_decay.reshape(span_count, ROWS, H)
    doc_spans = jnp.repeat(doc_ids, BLOCK).reshape(span_count, ROWS).astype(jnp.int32)
    prev_docs = jnp.concatenate([jnp.full((1,), -1, jnp.int32), doc_spans[:-1, -1].astype(jnp.int32)])

    def backward_span(incoming, pieces):
        query_c, key_c, value_c, grad_c, decay_c, doc_c, prev_c = pieces
        key_inner, value_inner, state, factor, weight_in = span_terms(query_c, key_c, value_c, grad_c, decay_c, doc_c, prev_c, True)
        key_grad, value_grad = apply_state(incoming, key_c, value_c, weight_in, key_inner, value_inner, True)
        return state + factor[:, None, None] * incoming, (key_grad, value_grad)

    start_state = jnp.zeros((H, DH, DH), jnp.float32)
    _, (key_grad, value_grad) = lax.scan(backward_span, start_state, (query_spans, key_spans, value_spans, grad_spans, decay_spans, doc_spans, prev_docs), reverse=True)
    return key_grad.reshape(SEQ, feature_count), value_grad.reshape(SEQ, feature_count)
```

```python
import functools

import jax
import jax.numpy as jnp
from jax import lax
from jax.experimental import pallas as pl
from jax.experimental.pallas import tpu as pltpu
from jax.sharding import PartitionSpec as P

BLOCK = 64
DH = 128
MESH = pl.DeviceIdType.MESH


def dot(a, b, dims):
    return lax.dot_general(a, b, (dims, ((), ())), preferred_element_type=jnp.float32)


NN = ((1,), (0,))
NT = ((1,), (1,))


def kernel(ctx_count, heads, docs, decay, q_hbm, k_hbm, v_hbm, og_hbm, dk, dv,
           q, k, v, g, cum, lead_row, tail_row, factor, factor_other, mine, other, sent, later,
           load_sem, swap_sem, fac_sem, pair_send, pair_recv, chain_send, chain_recv):
    rows = q.shape[0]
    half = og_hbm.shape[0]
    width = q.shape[1]
    group, ctx, tp = lax.axis_index("group"), lax.axis_index("ctx"), lax.axis_index("tp")
    odd = lax.rem(ctx, 2)
    pair = (group, ctx + 1 - 2 * odd, tp)
    core = (group, ctx, 1 - tp)
    before = (group, ctx - 2, tp)
    after = (group, ctx + 2, tp)
    has_before = ctx >= 2
    has_after = ctx < ctx_count - 2

    loads = [pltpu.make_async_copy(src, dst, load_sem.at[i])
             for i, (src, dst) in enumerate(((q_hbm, q), (k_hbm, k), (v_hbm, v)))]
    own_rows = pl.ds(pl.multiple_of(tp * half, half), half)
    loads.append(pltpu.make_async_copy(
        og_hbm.at[:, pl.ds(pl.multiple_of(tp * width, width), width)], g.at[own_rows, :], load_sem.at[3]))
    for copy in loads:
        copy.start()

    barrier = pltpu.get_barrier_semaphore()
    for peer in (pair, core):
        pl.semaphore_signal(barrier, inc=1, device_id=peer, device_id_type=MESH)

    @pl.when(has_before)
    def _():
        pl.semaphore_signal(barrier, inc=1, device_id=before, device_id_type=MESH)

    @pl.when(has_after)
    def _():
        pl.semaphore_signal(barrier, inc=1, device_id=after, device_id_type=MESH)

    pl.semaphore_wait(barrier, 2 + has_before.astype(jnp.int32) + has_after.astype(jnp.int32))

    swap = pltpu.make_async_remote_copy(
        src_ref=og_hbm.at[:, pl.ds(pl.multiple_of((1 - tp) * width, width), width)],
        dst_ref=g.at[own_rows, :], send_sem=swap_sem.at[0], recv_sem=swap_sem.at[1],
        device_id=core, device_id_type=MESH)
    swap.start()

    blocks = rows // BLOCK
    doc_list = [docs[ctx * blocks + b] for b in range(blocks)]
    first, last = doc_list[0], doc_list[-1]
    prev = docs[jnp.maximum(ctx * blocks - 1, 0)]
    linked = jnp.where((ctx > 0) & (prev == first), 1.0, 0.0).astype(jnp.float32)
    through = jnp.where(first == last, linked, 0.0).astype(jnp.float32)

    def doc_of(position):
        doc = jnp.full(position.shape, first, jnp.int32)
        for b in range(1, blocks):
            doc = jnp.where(position >= b * BLOCK, doc_list[b], doc)
        return doc

    lane = lax.broadcasted_iota(jnp.int32, (heads, rows), 1)
    total = decay[...]
    step = 1
    while step < rows:
        total = total + jnp.where(lane >= step, pltpu.roll(total, step, 1), 0.0)
        step *= 2
    lane_doc = doc_of(lane)
    ending = jnp.broadcast_to(total[:, rows - 1:rows], (heads, rows))
    cum[...] = total
    lead_row[...] = jnp.where(lane_doc == first, jnp.exp(total) * linked, 0.0)
    tail_row[...] = jnp.where(lane_doc == last, jnp.exp(ending - total), 0.0)
    factor[...] = jnp.exp(ending) * through
    fac_copy = pltpu.make_async_remote_copy(
        src_ref=factor, dst_ref=factor_other, send_sem=fac_sem.at[0], recv_sem=fac_sem.at[1],
        device_id=pair, device_id_type=MESH)
    fac_copy.start()

    def pair_copy(h):
        return pltpu.make_async_remote_copy(
            src_ref=mine.at[h], dst_ref=other.at[h], send_sem=pair_send.at[h], recv_sem=pair_recv.at[h],
            device_id=pair, device_id_type=MESH)

    def chain_copy(h):
        return pltpu.make_async_remote_copy(
            src_ref=sent.at[h], dst_ref=later.at[h], send_sem=chain_send.at[h], recv_sem=chain_recv.at[h],
            device_id=before, device_id_type=MESH)

    def columns(h):
        return pl.ds(pl.multiple_of(h * DH, DH), DH)

    for copy in loads:
        copy.wait()
    swap.wait()

    def state_step(h, carry):
        turned = q[:, columns(h)].astype(jnp.float32).T
        scaled = (turned * lead_row[pl.ds(h, 1), :]).astype(jnp.bfloat16)
        mine[h] = dot(scaled, g[:, columns(h)], NN).astype(mine.dtype)
        pair_copy(h).start()
        return carry

    lax.fori_loop(0, heads, state_step, 0, unroll=2)
    fac_copy.wait()

    key_at = lax.broadcasted_iota(jnp.int32, (rows, rows), 0)
    query_at = lax.broadcasted_iota(jnp.int32, (rows, rows), 1)
    allowed = (query_at >= key_at) & (doc_of(query_at) == doc_of(key_at))
    even = odd == 0

    def head_step(h, carry):
        cols = columns(h)
        qh, kh, vh, gh = q[:, cols], k[:, cols], v[:, cols], g[:, cols]
        along = jnp.broadcast_to(cum[pl.ds(h, 1), :], (rows, rows))
        weight = jnp.where(allowed, jnp.exp(jnp.minimum(along - along.T, 0.0)), 0.0)
        mixed_gv = (weight * dot(vh, gh, NT)).astype(jnp.bfloat16)
        mixed_qk = (weight * dot(kh, qh, NT)).astype(jnp.bfloat16)
        key_inner = dot(mixed_gv, qh, NN)
        value_inner = dot(mixed_qk, gh, NN)
        scale = jnp.broadcast_to(tail_row[pl.ds(h, 1), :], (rows, rows)).T

        pair_copy(h).wait_recv()
        own_state, pair_state = mine[h].astype(jnp.float32), other[h].astype(jnp.float32)
        own_factor, pair_factor = factor[pl.ds(h, 1), :], factor_other[pl.ds(h, 1), :]
        state_even = jnp.where(even, own_state, pair_state)
        state_odd = jnp.where(even, pair_state, own_state)
        factor_even = jnp.where(even, own_factor, pair_factor)

        @pl.when(has_after)
        def _():
            chain_copy(h).wait_recv()

        incoming = jnp.where(has_after, later[h].astype(jnp.float32), 0.0)

        @pl.when(has_before)
        def _():
            sent[h] = (state_even + factor_even * state_odd
                       + (own_factor * pair_factor) * incoming).astype(sent.dtype)
            chain_copy(h).start()

        state_in = jnp.where(even, pair_state + pair_factor * incoming, incoming).astype(jnp.bfloat16)
        dk[:, cols] = (key_inner + scale * dot(vh, state_in, NT)).astype(dk.dtype)
        dv[:, cols] = (value_inner + scale * dot(kh, state_in, NN)).astype(dv.dtype)
        return carry

    lax.fori_loop(0, heads, head_step, 0)

    def drain(h, carry):
        pair_copy(h).wait_send()

        @pl.when(has_before)
        def _():
            chain_copy(h).wait_send()

        return carry

    lax.fori_loop(0, heads, drain, 0)


def solution(mesh):
    ctx_count = mesh.shape["ctx"]
    wire = jnp.bfloat16 if ctx_count <= 8 else jnp.float32

    def per_device(queries, key_rows, value_rows, out_grad, log_decay, doc_ids):
        rows, features = queries.shape
        heads = log_decay.shape[1]
        anywhere = pl.BlockSpec(memory_space=pl.ANY)
        in_vmem = pl.BlockSpec(memory_space=pltpu.VMEM)
        wide = pltpu.VMEM((rows, features), jnp.bfloat16)
        small = pltpu.VMEM((heads, rows), jnp.float32)
        states = pltpu.VMEM((heads, DH, DH), wire)
        many = pltpu.SemaphoreType.DMA((heads,))
        shape = jax.ShapeDtypeStruct((rows, features), jnp.bfloat16)
        return tuple(pl.pallas_call(
            functools.partial(kernel, ctx_count, heads),
            out_shape=(shape, shape),
            in_specs=[pl.BlockSpec(memory_space=pltpu.SMEM), in_vmem] + [anywhere] * 4,
            out_specs=(in_vmem, in_vmem),
            scratch_shapes=[wide] * 4 + [small] * 5 + [states] * 4 + [
                pltpu.SemaphoreType.DMA((4,)), pltpu.SemaphoreType.DMA((2,)), pltpu.SemaphoreType.DMA((2,)),
                many, many, many, many],
            compiler_params=pltpu.CompilerParams(
                collective_id=0, has_side_effects=True, vmem_limit_bytes=63 << 20),
        )(doc_ids, log_decay.T, queries, key_rows, value_rows, out_grad))

    placed = (
        P(("group", "ctx"), "tp"),
        P(("group", "ctx"), "tp"),
        P(("group", "ctx"), "tp"),
        P(("group", "ctx", "tp"), None),
        P(("group", "ctx"), "tp"),
        P("group"),
    )
    return jax.shard_map(
        per_device,
        mesh=mesh,
        in_specs=placed,
        out_specs=(P(("group", "ctx"), "tp"), P(("group", "ctx"), "tp")),
        check_vma=False,
    )
```

```python
import functools

import jax
import jax.numpy as jnp
from jax import lax
from jax.experimental import pallas as pl
from jax.experimental.pallas import tpu as pltpu
from jax.sharding import PartitionSpec as P

BLOCK = 64
DH = 128
MESH = pl.DeviceIdType.MESH


def dot(a, b, dims):
    return lax.dot_general(a, b, (dims, ((), ())), preferred_element_type=jnp.float32)


NN = ((1,), (0,))
NT = ((1,), (1,))


def kernel(ctx_count, heads, docs, decay, q_hbm, k_hbm, v_hbm, og_hbm, dk, dv,
           q, k, v, g, cum, lead_row, tail_row, factor, factor_other, mine, given, other, sent, later,
           handed, back, key_inner, value_inner, allowed,
           load_sem, swap_sem, fac_sem, pair_send, pair_recv, chain_send, chain_recv, back_send, back_recv):
    rows = q.shape[0]
    half = og_hbm.shape[0]
    width = q.shape[1]
    group, ctx, tp = lax.axis_index("group"), lax.axis_index("ctx"), lax.axis_index("tp")
    odd = lax.rem(ctx, 2)
    pair = (group, ctx + 1 - 2 * odd, tp)
    core = (group, ctx, 1 - tp)
    before = (group, ctx - 2, tp)
    after = (group, ctx + 2, tp)
    has_before = ctx >= 2
    has_after = ctx < ctx_count - 2

    loads = [pltpu.make_async_copy(src, dst, load_sem.at[i])
             for i, (src, dst) in enumerate(((q_hbm, q), (k_hbm, k), (v_hbm, v)))]
    own_rows = pl.ds(pl.multiple_of(tp * half, half), half)
    loads.append(pltpu.make_async_copy(
        og_hbm.at[:, pl.ds(pl.multiple_of(tp * width, width), width)], g.at[own_rows, :], load_sem.at[3]))
    for copy in loads:
        copy.start()

    barrier = pltpu.get_barrier_semaphore()
    for peer in (pair, core):
        pl.semaphore_signal(barrier, inc=1, device_id=peer, device_id_type=MESH)

    @pl.when(has_before)
    def _():
        pl.semaphore_signal(barrier, inc=1, device_id=before, device_id_type=MESH)

    @pl.when(has_after)
    def _():
        pl.semaphore_signal(barrier, inc=1, device_id=after, device_id_type=MESH)

    pl.semaphore_wait(barrier, 2 + has_before.astype(jnp.int32) + has_after.astype(jnp.int32))

    swap = pltpu.make_async_remote_copy(
        src_ref=og_hbm.at[:, pl.ds(pl.multiple_of((1 - tp) * width, width), width)],
        dst_ref=g.at[own_rows, :], send_sem=swap_sem.at[0], recv_sem=swap_sem.at[1],
        device_id=core, device_id_type=MESH)
    swap.start()

    blocks = rows // BLOCK
    doc_list = [docs[ctx * blocks + b] for b in range(blocks)]
    first, last = doc_list[0], doc_list[-1]
    prev = docs[jnp.maximum(ctx * blocks - 1, 0)]
    linked = jnp.where((ctx > 0) & (prev == first), 1.0, 0.0).astype(jnp.float32)
    through = jnp.where(first == last, linked, 0.0).astype(jnp.float32)

    def doc_of(position):
        doc = jnp.full(position.shape, first, jnp.int32)
        for b in range(1, blocks):
            doc = jnp.where(position >= b * BLOCK, doc_list[b], doc)
        return doc

    lane = lax.broadcasted_iota(jnp.int32, (heads, rows), 1)
    total = decay[...]
    step = 1
    while step < rows:
        total = total + jnp.where(lane >= step, pltpu.roll(total, step, 1), 0.0)
        step *= 2
    lane_doc = doc_of(lane)
    ending = jnp.broadcast_to(total[:, rows - 1:rows], (heads, rows))
    cum[...] = total
    lead_row[...] = jnp.where(lane_doc == first, jnp.exp(total) * linked, 0.0)
    tail_row[...] = jnp.where(lane_doc == last, jnp.exp(ending - total), 0.0)
    factor[...] = jnp.exp(ending) * through
    fac_copy = pltpu.make_async_remote_copy(
        src_ref=factor, dst_ref=factor_other, send_sem=fac_sem.at[0], recv_sem=fac_sem.at[1],
        device_id=pair, device_id_type=MESH)
    fac_copy.start()

    half_heads = heads // 2
    own_base, pair_base = odd * half_heads, (1 - odd) * half_heads

    def pair_copy(i):
        return pltpu.make_async_remote_copy(
            src_ref=given.at[i], dst_ref=other.at[i], send_sem=pair_send.at[i], recv_sem=pair_recv.at[i],
            device_id=pair, device_id_type=MESH)

    def chain_copy(i):
        return pltpu.make_async_remote_copy(
            src_ref=sent.at[i], dst_ref=later.at[i], send_sem=chain_send.at[i], recv_sem=chain_recv.at[i],
            device_id=before, device_id_type=MESH)

    def back_copy(i):
        return pltpu.make_async_remote_copy(
            src_ref=handed.at[i], dst_ref=back.at[i], send_sem=back_send.at[i], recv_sem=back_recv.at[i],
            device_id=pair, device_id_type=MESH)

    def columns(h):
        return pl.ds(pl.multiple_of(h * DH, DH), DH)

    for copy in loads:
        copy.wait()
    swap.wait()

    def state_of(h):
        turned = q[:, columns(h)].astype(jnp.float32).T
        scaled = (turned * lead_row[pl.ds(h, 1), :]).astype(jnp.bfloat16)
        return dot(scaled, g[:, columns(h)], NN)

    def give_step(i, carry):
        given[i] = state_of(pair_base + i).astype(given.dtype)
        pair_copy(i).start()
        return carry

    def keep_step(i, carry):
        mine[i] = state_of(own_base + i)
        return carry

    lax.fori_loop(0, half_heads, give_step, 0, unroll=2)
    lax.fori_loop(0, half_heads, keep_step, 0, unroll=4)
    fac_copy.wait()

    key_at = lax.broadcasted_iota(jnp.int32, (rows, rows), 0)
    query_at = lax.broadcasted_iota(jnp.int32, (rows, rows), 1)
    allowed[...] = jnp.where(
        (query_at >= key_at) & (doc_of(query_at) == doc_of(key_at)), 1.0, 0.0)
    even = odd == 0

    def inner(h):
        cols = columns(h)
        qh, gh = q[:, cols], g[:, cols]
        along = jnp.broadcast_to(cum[pl.ds(h, 1), :], (rows, rows))
        weight = allowed[...] * jnp.exp(jnp.minimum(along - along.T, 0.0))
        mixed_gv = (weight * dot(v[:, cols], gh, NT)).astype(jnp.bfloat16)
        mixed_qk = (weight * dot(k[:, cols], qh, NT)).astype(jnp.bfloat16)
        key_inner[:, cols] = dot(mixed_gv, qh, NN)
        value_inner[:, cols] = dot(mixed_qk, gh, NN)

    def apply(h, state_in):
        cols = columns(h)
        scale = jnp.broadcast_to(tail_row[pl.ds(h, 1), :], (rows, rows)).T
        dk[:, cols] = (key_inner[:, cols] + scale * dot(v[:, cols], state_in, NT)).astype(dk.dtype)
        dv[:, cols] = (value_inner[:, cols] + scale * dot(k[:, cols], state_in, NN)).astype(dv.dtype)

    def chain_step(i, carry):
        h = own_base + i
        inner(h)
        inner(pair_base + i)
        pair_copy(i).wait_recv()
        own_state, pair_state = mine[i], other[i].astype(jnp.float32)
        own_factor, pair_factor = factor[pl.ds(h, 1), :], factor_other[pl.ds(h, 1), :]
        state_even = jnp.where(even, own_state, pair_state)
        state_odd = jnp.where(even, pair_state, own_state)
        factor_even = jnp.where(even, own_factor, pair_factor)
        factor_odd = jnp.where(even, pair_factor, own_factor)
        joined = state_even + factor_even * state_odd

        @pl.when(has_after)
        def _():
            chain_copy(i).wait_recv()

        incoming = jnp.where(has_after, later[i].astype(jnp.float32), 0.0)

        @pl.when(has_before)
        def _():
            sent[i] = (joined + (factor_even * factor_odd) * incoming).astype(sent.dtype)
            chain_copy(i).start()

        into_even = (state_odd + factor_odd * incoming).astype(jnp.bfloat16)
        into_odd = incoming.astype(jnp.bfloat16)
        handed[i] = jnp.where(even, into_odd, into_even)
        back_copy(i).start()
        apply(h, jnp.where(even, into_even, into_odd))
        return carry

    lax.fori_loop(0, half_heads, chain_step, 0)

    def last_step(i, carry):
        back_copy(i).wait_recv()
        apply(pair_base + i, back[i])
        return carry

    lax.fori_loop(0, half_heads, last_step, 0)

    def drain(i, carry):
        pair_copy(i).wait_send()
        back_copy(i).wait_send()

        @pl.when(has_before)
        def _():
            chain_copy(i).wait_send()

        return carry

    lax.fori_loop(0, half_heads, drain, 0)


def solution(mesh):
    ctx_count = mesh.shape["ctx"]
    wire = jnp.bfloat16 if ctx_count <= 8 else jnp.float32

    def per_device(queries, key_rows, value_rows, out_grad, log_decay, doc_ids):
        rows, features = queries.shape
        heads = log_decay.shape[1]
        anywhere = pl.BlockSpec(memory_space=pl.ANY)
        in_vmem = pl.BlockSpec(memory_space=pltpu.VMEM)
        wide = pltpu.VMEM((rows, features), jnp.bfloat16)
        small = pltpu.VMEM((heads, rows), jnp.float32)
        half = heads // 2
        states = pltpu.VMEM((half, DH, DH), wire)
        kept = pltpu.VMEM((half, DH, DH), jnp.float32)
        rounded = pltpu.VMEM((half, DH, DH), jnp.bfloat16)
        total = pltpu.VMEM((rows, features), jnp.float32)
        square = pltpu.VMEM((rows, rows), jnp.float32)
        many = pltpu.SemaphoreType.DMA((half,))
        shape = jax.ShapeDtypeStruct((rows, features), jnp.bfloat16)
        return tuple(pl.pallas_call(
            functools.partial(kernel, ctx_count, heads),
            out_shape=(shape, shape),
            in_specs=[pl.BlockSpec(memory_space=pltpu.SMEM), in_vmem] + [anywhere] * 4,
            out_specs=(in_vmem, in_vmem),
            scratch_shapes=[wide] * 4 + [small] * 5 + [kept] + [states] * 4 + [rounded] * 2 + [total] * 2 + [square] + [
                pltpu.SemaphoreType.DMA((4,)), pltpu.SemaphoreType.DMA((2,)), pltpu.SemaphoreType.DMA((2,)),
                many, many, many, many, many, many],
            compiler_params=pltpu.CompilerParams(
                collective_id=0, has_side_effects=True, vmem_limit_bytes=63 << 20),
        )(doc_ids, log_decay.T, queries, key_rows, value_rows, out_grad))

    placed = (
        P(("group", "ctx"), "tp"),
        P(("group", "ctx"), "tp"),
        P(("group", "ctx"), "tp"),
        P(("group", "ctx", "tp"), None),
        P(("group", "ctx"), "tp"),
        P("group"),
    )
    return jax.shard_map(
        per_device,
        mesh=mesh,
        in_specs=placed,
        out_specs=(P(("group", "ctx"), "tp"), P(("group", "ctx"), "tp")),
        check_vma=False,
    )
```

```python
import functools

import jax
import jax.numpy as jnp
from jax import lax
from jax.experimental import pallas as pl
from jax.experimental.pallas import tpu as pltpu
from jax.sharding import PartitionSpec as P

BLOCK = 64
DH = 128
MESH = pl.DeviceIdType.MESH


def dot(a, b, dims):
    return lax.dot_general(a, b, (dims, ((), ())), preferred_element_type=jnp.float32)


NN = ((1,), (0,))
NT = ((1,), (1,))


def kernel(ctx_count, heads, docs, decay, q_hbm, k_hbm, v_hbm, og_hbm, dk, dv,
           q, k, v, g, cum, lead_row, tail_row, factor, factor_other, mine, given, other, sent, later,
           handed, back, key_inner, value_inner, allowed,
           load_sem, swap_sem, fac_sem, pair_send, pair_recv, chain_send, chain_recv, back_send, back_recv):
    rows = q.shape[0]
    half = og_hbm.shape[0]
    width = q.shape[1]
    group, ctx, tp = lax.axis_index("group"), lax.axis_index("ctx"), lax.axis_index("tp")
    odd = lax.rem(ctx, 2)
    pair = (group, ctx + 1 - 2 * odd, tp)
    core = (group, ctx, 1 - tp)
    before = (group, ctx - 2, tp)
    after = (group, ctx + 2, tp)
    has_before = ctx >= 2
    has_after = ctx < ctx_count - 2

    loads = [pltpu.make_async_copy(src, dst, load_sem.at[i])
             for i, (src, dst) in enumerate(((q_hbm, q), (k_hbm, k), (v_hbm, v)))]
    own_rows = pl.ds(pl.multiple_of(tp * half, half), half)
    loads.append(pltpu.make_async_copy(
        og_hbm.at[:, pl.ds(pl.multiple_of(tp * width, width), width)], g.at[own_rows, :], load_sem.at[3]))
    for copy in loads:
        copy.start()

    barrier = pltpu.get_barrier_semaphore()
    for peer in (pair, core):
        pl.semaphore_signal(barrier, inc=1, device_id=peer, device_id_type=MESH)

    @pl.when(has_before)
    def _():
        pl.semaphore_signal(barrier, inc=1, device_id=before, device_id_type=MESH)

    @pl.when(has_after)
    def _():
        pl.semaphore_signal(barrier, inc=1, device_id=after, device_id_type=MESH)

    pl.semaphore_wait(barrier, 2 + has_before.astype(jnp.int32) + has_after.astype(jnp.int32))

    swap = pltpu.make_async_remote_copy(
        src_ref=og_hbm.at[:, pl.ds(pl.multiple_of((1 - tp) * width, width), width)],
        dst_ref=g.at[own_rows, :], send_sem=swap_sem.at[0], recv_sem=swap_sem.at[1],
        device_id=core, device_id_type=MESH)
    swap.start()

    blocks = rows // BLOCK
    doc_list = [docs[ctx * blocks + b] for b in range(blocks)]
    first, last = doc_list[0], doc_list[-1]
    prev = docs[jnp.maximum(ctx * blocks - 1, 0)]
    linked = jnp.where((ctx > 0) & (prev == first), 1.0, 0.0).astype(jnp.float32)
    through = jnp.where(first == last, linked, 0.0).astype(jnp.float32)

    def doc_of(position):
        doc = jnp.full(position.shape, first, jnp.int32)
        for b in range(1, blocks):
            doc = jnp.where(position >= b * BLOCK, doc_list[b], doc)
        return doc

    lane = lax.broadcasted_iota(jnp.int32, (heads, rows), 1)
    total = decay[...]
    step = 1
    while step < rows:
        total = total + jnp.where(lane >= step, pltpu.roll(total, step, 1), 0.0)
        step *= 2
    lane_doc = doc_of(lane)
    ending = jnp.broadcast_to(total[:, rows - 1:rows], (heads, rows))
    cum[...] = total
    lead_row[...] = jnp.where(lane_doc == first, jnp.exp(total) * linked, 0.0)
    tail_row[...] = jnp.where(lane_doc == last, jnp.exp(ending - total), 0.0)
    factor[...] = jnp.exp(ending) * through
    fac_copy = pltpu.make_async_remote_copy(
        src_ref=factor, dst_ref=factor_other, send_sem=fac_sem.at[0], recv_sem=fac_sem.at[1],
        device_id=pair, device_id_type=MESH)
    fac_copy.start()

    half_heads = heads // 2
    own_base, pair_base = odd * half_heads, (1 - odd) * half_heads

    def pair_copy(i):
        return pltpu.make_async_remote_copy(
            src_ref=given.at[i], dst_ref=other.at[i], send_sem=pair_send.at[i], recv_sem=pair_recv.at[i],
            device_id=pair, device_id_type=MESH)

    def chain_copy(i):
        return pltpu.make_async_remote_copy(
            src_ref=sent.at[i], dst_ref=later.at[i], send_sem=chain_send.at[i], recv_sem=chain_recv.at[i],
            device_id=before, device_id_type=MESH)

    def back_copy(i):
        return pltpu.make_async_remote_copy(
            src_ref=handed.at[i], dst_ref=back.at[i], send_sem=back_send.at[i], recv_sem=back_recv.at[i],
            device_id=pair, device_id_type=MESH)

    def columns(h):
        return pl.ds(pl.multiple_of(h * DH, DH), DH)

    for copy in loads:
        copy.wait()
    swap.wait()

    def state_of(h):
        turned = q[:, columns(h)].astype(jnp.float32).T
        scaled = (turned * lead_row[pl.ds(h, 1), :]).astype(jnp.bfloat16)
        return dot(scaled, g[:, columns(h)], NN)

    def give_step(i, carry):
        for j in range(2):
            given[2 * i + j] = state_of(pair_base + 2 * i + j).astype(given.dtype)
        for j in range(2):
            pair_copy(2 * i + j).start()
        return carry

    def keep_step(i, carry):
        mine[i] = state_of(own_base + i)
        return carry

    lax.fori_loop(0, half_heads // 2, give_step, 0)
    lax.fori_loop(0, half_heads, keep_step, 0, unroll=4)
    fac_copy.wait()

    key_at = lax.broadcasted_iota(jnp.int32, (rows, rows), 0)
    query_at = lax.broadcasted_iota(jnp.int32, (rows, rows), 1)
    allowed[...] = jnp.where(
        (query_at >= key_at) & (doc_of(query_at) == doc_of(key_at)), 1.0, 0.0)
    even = odd == 0

    def inner(h):
        cols = columns(h)
        qh, gh = q[:, cols], g[:, cols]
        along = jnp.broadcast_to(cum[pl.ds(h, 1), :], (rows, rows))
        weight = allowed[...] * jnp.exp(jnp.minimum(along - along.T, 0.0))
        mixed_gv = (weight * dot(v[:, cols], gh, NT)).astype(jnp.bfloat16)
        mixed_qk = (weight * dot(k[:, cols], qh, NT)).astype(jnp.bfloat16)
        key_inner[:, cols] = dot(mixed_gv, qh, NN)
        value_inner[:, cols] = dot(mixed_qk, gh, NN)

    def apply(h, state_in):
        cols = columns(h)
        scale = jnp.broadcast_to(tail_row[pl.ds(h, 1), :], (rows, rows)).T
        dk[:, cols] = (key_inner[:, cols] + scale * dot(v[:, cols], state_in, NT)).astype(dk.dtype)
        dv[:, cols] = (value_inner[:, cols] + scale * dot(k[:, cols], state_in, NN)).astype(dv.dtype)

    def chain_step(i, carry):
        h = own_base + i
        pair_copy(i).wait_recv()
        own_state, pair_state = mine[i], other[i].astype(jnp.float32)
        own_factor, pair_factor = factor[pl.ds(h, 1), :], factor_other[pl.ds(h, 1), :]
        state_even = jnp.where(even, own_state, pair_state)
        state_odd = jnp.where(even, pair_state, own_state)
        factor_even = jnp.where(even, own_factor, pair_factor)
        factor_odd = jnp.where(even, pair_factor, own_factor)
        joined = state_even + factor_even * state_odd

        @pl.when(has_after)
        def _():
            chain_copy(i).wait_recv()

        incoming = jnp.where(has_after, later[i].astype(jnp.float32), 0.0)

        @pl.when(has_before)
        def _():
            sent[i] = (joined + (factor_even * factor_odd) * incoming).astype(sent.dtype)
            chain_copy(i).start()

        into_even = (state_odd + factor_odd * incoming).astype(jnp.bfloat16)
        into_odd = incoming.astype(jnp.bfloat16)
        handed[i] = jnp.where(even, into_odd, into_even)
        back_copy(i).start()
        inner(pair_base + i)
        apply(h, jnp.where(even, into_even, into_odd))
        return carry

    def early_step(i, carry):
        inner(own_base + i)
        return carry

    lax.fori_loop(0, half_heads, early_step, 0, unroll=4)
    lax.fori_loop(0, half_heads, chain_step, 0)

    def last_step(i, carry):
        back_copy(i).wait_recv()
        apply(pair_base + i, back[i])
        return carry

    lax.fori_loop(0, half_heads, last_step, 0)

    def drain(i, carry):
        pair_copy(i).wait_send()
        back_copy(i).wait_send()

        @pl.when(has_before)
        def _():
            chain_copy(i).wait_send()

        return carry

    lax.fori_loop(0, half_heads, drain, 0)


def solution(mesh):
    ctx_count = mesh.shape["ctx"]
    wire = jnp.bfloat16 if ctx_count <= 8 else jnp.float32

    def per_device(queries, key_rows, value_rows, out_grad, log_decay, doc_ids):
        rows, features = queries.shape
        heads = log_decay.shape[1]
        anywhere = pl.BlockSpec(memory_space=pl.ANY)
        in_vmem = pl.BlockSpec(memory_space=pltpu.VMEM)
        wide = pltpu.VMEM((rows, features), jnp.bfloat16)
        small = pltpu.VMEM((heads, rows), jnp.float32)
        half = heads // 2
        states = pltpu.VMEM((half, DH, DH), wire)
        kept = pltpu.VMEM((half, DH, DH), jnp.float32)
        rounded = pltpu.VMEM((half, DH, DH), jnp.bfloat16)
        total = pltpu.VMEM((rows, features), jnp.float32)
        square = pltpu.VMEM((rows, rows), jnp.float32)
        many = pltpu.SemaphoreType.DMA((half,))
        shape = jax.ShapeDtypeStruct((rows, features), jnp.bfloat16)
        return tuple(pl.pallas_call(
            functools.partial(kernel, ctx_count, heads),
            out_shape=(shape, shape),
            in_specs=[pl.BlockSpec(memory_space=pltpu.SMEM), in_vmem] + [anywhere] * 4,
            out_specs=(in_vmem, in_vmem),
            scratch_shapes=[wide] * 4 + [small] * 5 + [kept] + [states] * 4 + [rounded] * 2 + [total] * 2 + [square] + [
                pltpu.SemaphoreType.DMA((4,)), pltpu.SemaphoreType.DMA((2,)), pltpu.SemaphoreType.DMA((2,)),
                many, many, many, many, many, many],
            compiler_params=pltpu.CompilerParams(
                collective_id=0, has_side_effects=True, vmem_limit_bytes=63 << 20),
        )(doc_ids, log_decay.T, queries, key_rows, value_rows, out_grad))

    placed = (
        P(("group", "ctx"), "tp"),
        P(("group", "ctx"), "tp"),
        P(("group", "ctx"), "tp"),
        P(("group", "ctx", "tp"), None),
        P(("group", "ctx"), "tp"),
        P("group"),
    )
    return jax.shard_map(
        per_device,
        mesh=mesh,
        in_specs=placed,
        out_specs=(P(("group", "ctx"), "tp"), P(("group", "ctx"), "tp")),
        check_vma=False,
    )
```

```python
import functools

import jax
import jax.numpy as jnp
from jax import lax
from jax.experimental import pallas as pl
from jax.experimental.pallas import tpu as pltpu
from jax.sharding import PartitionSpec as P

BLOCK = 64
DH = 128
MESH = pl.DeviceIdType.MESH


def dot(a, b, dims):
    return lax.dot_general(a, b, (dims, ((), ())), preferred_element_type=jnp.float32)


NN = ((1,), (0,))
NT = ((1,), (1,))


def kernel(ctx_count, heads, docs, decay, q_hbm, k_hbm, v_hbm, og_hbm, dk_hbm, dv_hbm,
           dk, dv, q, k, v, g, cum, lead_row, tail_row, factor, factor_other, mine, given, other, sent, later,
           handed, back, key_inner, value_inner, allowed,
           load_sem, swap_sem, fac_sem, pair_send, pair_recv, chain_send, chain_recv, back_send, back_recv, out_sem):
    rows = q.shape[0]
    half = og_hbm.shape[0]
    width = q.shape[1]
    group, ctx, tp = lax.axis_index("group"), lax.axis_index("ctx"), lax.axis_index("tp")
    odd = lax.rem(ctx, 2)
    pair = (group, ctx + 1 - 2 * odd, tp)
    core = (group, ctx, 1 - tp)
    before = (group, ctx - 2, tp)
    after = (group, ctx + 2, tp)
    has_before = ctx >= 2
    has_after = ctx < ctx_count - 2

    loads = [pltpu.make_async_copy(src, dst, load_sem.at[i])
             for i, (src, dst) in enumerate(((q_hbm, q), (k_hbm, k), (v_hbm, v)))]
    own_rows = pl.ds(pl.multiple_of(tp * half, half), half)
    loads.append(pltpu.make_async_copy(
        og_hbm.at[:, pl.ds(pl.multiple_of(tp * width, width), width)], g.at[own_rows, :], load_sem.at[3]))
    for copy in loads:
        copy.start()

    barrier = pltpu.get_barrier_semaphore()
    for peer in (pair, core):
        pl.semaphore_signal(barrier, inc=1, device_id=peer, device_id_type=MESH)

    @pl.when(has_before)
    def _():
        pl.semaphore_signal(barrier, inc=1, device_id=before, device_id_type=MESH)

    @pl.when(has_after)
    def _():
        pl.semaphore_signal(barrier, inc=1, device_id=after, device_id_type=MESH)

    pl.semaphore_wait(barrier, 2 + has_before.astype(jnp.int32) + has_after.astype(jnp.int32))

    swap = pltpu.make_async_remote_copy(
        src_ref=og_hbm.at[:, pl.ds(pl.multiple_of((1 - tp) * width, width), width)],
        dst_ref=g.at[own_rows, :], send_sem=swap_sem.at[0], recv_sem=swap_sem.at[1],
        device_id=core, device_id_type=MESH)
    swap.start()

    blocks = rows // BLOCK
    doc_list = [docs[ctx * blocks + b] for b in range(blocks)]
    first, last = doc_list[0], doc_list[-1]
    prev = docs[jnp.maximum(ctx * blocks - 1, 0)]
    linked = jnp.where((ctx > 0) & (prev == first), 1.0, 0.0).astype(jnp.float32)
    through = jnp.where(first == last, linked, 0.0).astype(jnp.float32)

    def doc_of(position):
        doc = jnp.full(position.shape, first, jnp.int32)
        for b in range(1, blocks):
            doc = jnp.where(position >= b * BLOCK, doc_list[b], doc)
        return doc

    lane = lax.broadcasted_iota(jnp.int32, (heads, rows), 1)
    total = decay[...]
    step = 1
    while step < rows:
        total = total + jnp.where(lane >= step, pltpu.roll(total, step, 1), 0.0)
        step *= 2
    lane_doc = doc_of(lane)
    ending = jnp.broadcast_to(total[:, rows - 1:rows], (heads, rows))
    cum[...] = total
    lead_row[...] = jnp.where(lane_doc == first, jnp.exp(total) * linked, 0.0)
    tail_row[...] = jnp.where(lane_doc == last, jnp.exp(ending - total), 0.0)
    factor[...] = jnp.exp(ending) * through
    fac_copy = pltpu.make_async_remote_copy(
        src_ref=factor, dst_ref=factor_other, send_sem=fac_sem.at[0], recv_sem=fac_sem.at[1],
        device_id=pair, device_id_type=MESH)
    fac_copy.start()

    half_heads = heads // 2
    own_base, pair_base = odd * half_heads, (1 - odd) * half_heads

    def pair_copy(i):
        return pltpu.make_async_remote_copy(
            src_ref=given.at[i], dst_ref=other.at[i], send_sem=pair_send.at[i], recv_sem=pair_recv.at[i],
            device_id=pair, device_id_type=MESH)

    def chain_copy(i):
        return pltpu.make_async_remote_copy(
            src_ref=sent.at[i], dst_ref=later.at[i], send_sem=chain_send.at[i], recv_sem=chain_recv.at[i],
            device_id=before, device_id_type=MESH)

    def back_copy(i):
        return pltpu.make_async_remote_copy(
            src_ref=handed.at[i], dst_ref=back.at[i], send_sem=back_send.at[i], recv_sem=back_recv.at[i],
            device_id=pair, device_id_type=MESH)

    def columns(h):
        return pl.ds(pl.multiple_of(h * DH, DH), DH)

    for copy in loads:
        copy.wait()
    swap.wait()

    def state_of(h):
        turned = q[:, columns(h)].astype(jnp.float32).T
        scaled = (turned * lead_row[pl.ds(h, 1), :]).astype(jnp.bfloat16)
        return dot(scaled, g[:, columns(h)], NN)

    def give_step(i, carry):
        for j in range(2):
            given[2 * i + j] = state_of(pair_base + 2 * i + j).astype(given.dtype)
        for j in range(2):
            pair_copy(2 * i + j).start()
        return carry

    def keep_step(i, carry):
        mine[i] = state_of(own_base + i)
        return carry

    lax.fori_loop(0, half_heads // 2, give_step, 0)
    lax.fori_loop(0, half_heads, keep_step, 0, unroll=4)
    fac_copy.wait()

    key_at = lax.broadcasted_iota(jnp.int32, (rows, rows), 0)
    query_at = lax.broadcasted_iota(jnp.int32, (rows, rows), 1)
    allowed[...] = jnp.where(
        (query_at >= key_at) & (doc_of(query_at) == doc_of(key_at)), 1.0, 0.0)
    even = odd == 0

    def inner(h):
        cols = columns(h)
        qh, gh = q[:, cols], g[:, cols]
        along = jnp.broadcast_to(cum[pl.ds(h, 1), :], (rows, rows))
        weight = allowed[...] * jnp.exp(jnp.minimum(along - along.T, 0.0))
        mixed_gv = (weight * dot(v[:, cols], gh, NT)).astype(jnp.bfloat16)
        mixed_qk = (weight * dot(k[:, cols], qh, NT)).astype(jnp.bfloat16)
        key_inner[:, cols] = dot(mixed_gv, qh, NN)
        value_inner[:, cols] = dot(mixed_qk, gh, NN)

    def out_copies(h):
        cols = columns(h)
        return (pltpu.make_async_copy(dk.at[:, cols], dk_hbm.at[:, cols], out_sem.at[0, h]),
                pltpu.make_async_copy(dv.at[:, cols], dv_hbm.at[:, cols], out_sem.at[1, h]))

    def apply(h, state_in):
        cols = columns(h)
        scale = jnp.broadcast_to(tail_row[pl.ds(h, 1), :], (rows, rows)).T
        dk[:, cols] = (key_inner[:, cols] + scale * dot(v[:, cols], state_in, NT)).astype(dk.dtype)
        dv[:, cols] = (value_inner[:, cols] + scale * dot(k[:, cols], state_in, NN)).astype(dv.dtype)
        for copy in out_copies(h):
            copy.start()

    def chain_step(i, carry):
        h = own_base + i
        pair_copy(i).wait_recv()
        own_state, pair_state = mine[i], other[i].astype(jnp.float32)
        own_factor, pair_factor = factor[pl.ds(h, 1), :], factor_other[pl.ds(h, 1), :]
        state_even = jnp.where(even, own_state, pair_state)
        state_odd = jnp.where(even, pair_state, own_state)
        factor_even = jnp.where(even, own_factor, pair_factor)
        factor_odd = jnp.where(even, pair_factor, own_factor)
        joined = state_even + factor_even * state_odd

        @pl.when(has_after)
        def _():
            chain_copy(i).wait_recv()

        incoming = jnp.where(has_after, later[i].astype(jnp.float32), 0.0)

        @pl.when(has_before)
        def _():
            sent[i] = (joined + (factor_even * factor_odd) * incoming).astype(sent.dtype)
            chain_copy(i).start()

        into_even = (state_odd + factor_odd * incoming).astype(jnp.bfloat16)
        into_odd = incoming.astype(jnp.bfloat16)
        handed[i] = jnp.where(even, into_odd, into_even)
        back_copy(i).start()
        inner(pair_base + i)
        apply(h, jnp.where(even, into_even, into_odd))
        return carry

    def early_step(i, carry):
        inner(own_base + i)
        return carry

    lax.fori_loop(0, half_heads, early_step, 0, unroll=4)
    lax.fori_loop(0, half_heads, chain_step, 0)

    def last_step(i, carry):
        back_copy(i).wait_recv()
        apply(pair_base + i, back[i])
        return carry

    lax.fori_loop(0, half_heads, last_step, 0)

    def drain(i, carry):
        pair_copy(i).wait_send()
        back_copy(i).wait_send()
        for h in (i, half_heads + i):
            for copy in out_copies(h):
                copy.wait()

        @pl.when(has_before)
        def _():
            chain_copy(i).wait_send()

        return carry

    lax.fori_loop(0, half_heads, drain, 0)


def handover(a_in, b_in, a_out, b_out, a_buf, b_buf, in_sem, out_sem):
    pieces = a_buf.shape[0] // 32
    moves = []
    for i in range(pieces):
        part = pl.ds(32 * i, 32)
        for n, (src, buf, dst) in enumerate(((a_in, a_buf, a_out), (b_in, b_buf, b_out))):
            moves.append((pltpu.make_async_copy(src.at[part, :], buf.at[part, :], in_sem.at[n, i]),
                          pltpu.make_async_copy(buf.at[part, :], dst.at[part, :], out_sem.at[n, i])))
    for come, _ in moves:
        come.start()
    for come, go in moves:
        come.wait()
        go.start()
    for _, go in moves:
        go.wait()


def solution(mesh):
    ctx_count = mesh.shape["ctx"]
    wire = jnp.bfloat16 if ctx_count <= 8 else jnp.float32

    def per_device(queries, key_rows, value_rows, out_grad, log_decay, doc_ids):
        rows, features = queries.shape
        heads = log_decay.shape[1]
        anywhere = pl.BlockSpec(memory_space=pl.ANY)
        in_vmem = pl.BlockSpec(memory_space=pltpu.VMEM)
        wide = pltpu.VMEM((rows, features), jnp.bfloat16)
        small = pltpu.VMEM((heads, rows), jnp.float32)
        half = heads // 2
        states = pltpu.VMEM((half, DH, DH), wire)
        kept = pltpu.VMEM((half, DH, DH), jnp.float32)
        rounded = pltpu.VMEM((half, DH, DH), jnp.bfloat16)
        total = pltpu.VMEM((rows, features), jnp.float32)
        square = pltpu.VMEM((rows, rows), jnp.float32)
        many = pltpu.SemaphoreType.DMA((half,))
        shape = jax.ShapeDtypeStruct((rows, features), jnp.bfloat16)
        key_grad, value_grad = pl.pallas_call(
            functools.partial(kernel, ctx_count, heads),
            out_shape=(shape, shape),
            in_specs=[pl.BlockSpec(memory_space=pltpu.SMEM), in_vmem] + [anywhere] * 4,
            out_specs=(anywhere, anywhere),
            scratch_shapes=[wide] * 6 + [small] * 5 + [kept] + [states] * 4 + [rounded] * 2 + [total] * 2 + [square] + [
                pltpu.SemaphoreType.DMA((4,)), pltpu.SemaphoreType.DMA((2,)), pltpu.SemaphoreType.DMA((2,)),
                many, many, many, many, many, many, pltpu.SemaphoreType.DMA((2, heads))],
            compiler_params=pltpu.CompilerParams(
                collective_id=0, has_side_effects=True, vmem_limit_bytes=63 << 20),
        )(doc_ids, log_decay.T, queries, key_rows, value_rows, out_grad)
        pieces = pltpu.SemaphoreType.DMA((2, rows // 32))
        return tuple(pl.pallas_call(
            handover,
            out_shape=(shape, shape),
            in_specs=[anywhere] * 2,
            out_specs=(anywhere, anywhere),
            scratch_shapes=[wide, wide, pieces, pieces],
            compiler_params=pltpu.CompilerParams(vmem_limit_bytes=63 << 20),
        )(key_grad, value_grad))

    placed = (
        P(("group", "ctx"), "tp"),
        P(("group", "ctx"), "tp"),
        P(("group", "ctx"), "tp"),
        P(("group", "ctx", "tp"), None),
        P(("group", "ctx"), "tp"),
        P("group"),
    )
    return jax.shard_map(
        per_device,
        mesh=mesh,
        in_specs=placed,
        out_specs=(P(("group", "ctx"), "tp"), P(("group", "ctx"), "tp")),
        check_vma=False,
    )
```

```python
import functools

import jax
import jax.numpy as jnp
from jax import lax
from jax.experimental import pallas as pl
from jax.experimental.pallas import tpu as pltpu
from jax.sharding import PartitionSpec as P

BLOCK = 64
DH = 128
MESH = pl.DeviceIdType.MESH


def dot(a, b, dims):
    return lax.dot_general(a, b, (dims, ((), ())), preferred_element_type=jnp.float32)


NN = ((1,), (0,))
NT = ((1,), (1,))


def kernel(ctx_count, heads, docs, decay, q_hbm, k_hbm, v_hbm, og_hbm, dk_hbm, dv_hbm,
           dk, dv, q, k, v, g, cum, lead_row, tail_row, factor, factor_other, mine, given, other, sent, later,
           handed, back, held, key_inner, value_inner, allowed,
           load_sem, swap_sem, fac_sem, pair_send, pair_recv, chain_send, chain_recv, back_send, back_recv, out_sem):
    rows = q.shape[0]
    half = og_hbm.shape[0]
    width = q.shape[1]
    group, ctx, tp = lax.axis_index("group"), lax.axis_index("ctx"), lax.axis_index("tp")
    odd = lax.rem(ctx, 2)
    pair = (group, ctx + 1 - 2 * odd, tp)
    core = (group, ctx, 1 - tp)
    before = (group, ctx - 2, tp)
    after = (group, ctx + 2, tp)
    has_before = ctx >= 2
    has_after = ctx < ctx_count - 2

    loads = [pltpu.make_async_copy(src, dst, load_sem.at[i])
             for i, (src, dst) in enumerate(((q_hbm, q), (k_hbm, k), (v_hbm, v)))]
    own_rows = pl.ds(pl.multiple_of(tp * half, half), half)
    loads.append(pltpu.make_async_copy(
        og_hbm.at[:, pl.ds(pl.multiple_of(tp * width, width), width)], g.at[own_rows, :], load_sem.at[3]))
    for copy in loads:
        copy.start()

    barrier = pltpu.get_barrier_semaphore()
    for peer in (pair, core):
        pl.semaphore_signal(barrier, inc=1, device_id=peer, device_id_type=MESH)

    @pl.when(has_before)
    def _():
        pl.semaphore_signal(barrier, inc=1, device_id=before, device_id_type=MESH)

    @pl.when(has_after)
    def _():
        pl.semaphore_signal(barrier, inc=1, device_id=after, device_id_type=MESH)

    pl.semaphore_wait(barrier, 2 + has_before.astype(jnp.int32) + has_after.astype(jnp.int32))

    swap = pltpu.make_async_remote_copy(
        src_ref=og_hbm.at[:, pl.ds(pl.multiple_of((1 - tp) * width, width), width)],
        dst_ref=g.at[own_rows, :], send_sem=swap_sem.at[0], recv_sem=swap_sem.at[1],
        device_id=core, device_id_type=MESH)
    swap.start()

    blocks = rows // BLOCK
    doc_list = [docs[ctx * blocks + b] for b in range(blocks)]
    first, last = doc_list[0], doc_list[-1]
    prev = docs[jnp.maximum(ctx * blocks - 1, 0)]
    linked = jnp.where((ctx > 0) & (prev == first), 1.0, 0.0).astype(jnp.float32)
    through = jnp.where(first == last, linked, 0.0).astype(jnp.float32)

    def doc_of(position):
        doc = jnp.full(position.shape, first, jnp.int32)
        for b in range(1, blocks):
            doc = jnp.where(position >= b * BLOCK, doc_list[b], doc)
        return doc

    lane = lax.broadcasted_iota(jnp.int32, (heads, rows), 1)
    total = decay[...]
    step = 1
    while step < rows:
        total = total + jnp.where(lane >= step, pltpu.roll(total, step, 1), 0.0)
        step *= 2
    lane_doc = doc_of(lane)
    ending = jnp.broadcast_to(total[:, rows - 1:rows], (heads, rows))
    cum[...] = total
    lead_row[...] = jnp.where(lane_doc == first, jnp.exp(total) * linked, 0.0)
    tail_row[...] = jnp.where(lane_doc == last, jnp.exp(ending - total), 0.0)
    factor[...] = jnp.exp(ending) * through
    fac_copy = pltpu.make_async_remote_copy(
        src_ref=factor, dst_ref=factor_other, send_sem=fac_sem.at[0], recv_sem=fac_sem.at[1],
        device_id=pair, device_id_type=MESH)
    fac_copy.start()

    half_heads = heads // 2
    own_base, pair_base = odd * half_heads, (1 - odd) * half_heads

    def pair_copy(i):
        return pltpu.make_async_remote_copy(
            src_ref=given.at[i], dst_ref=other.at[i], send_sem=pair_send.at[i], recv_sem=pair_recv.at[i],
            device_id=pair, device_id_type=MESH)

    def chain_copy(i):
        return pltpu.make_async_remote_copy(
            src_ref=sent.at[i], dst_ref=later.at[i], send_sem=chain_send.at[i], recv_sem=chain_recv.at[i],
            device_id=before, device_id_type=MESH)

    def back_copy(i):
        return pltpu.make_async_remote_copy(
            src_ref=handed.at[i], dst_ref=back.at[i], send_sem=back_send.at[i], recv_sem=back_recv.at[i],
            device_id=pair, device_id_type=MESH)

    def columns(h):
        return pl.ds(pl.multiple_of(h * DH, DH), DH)

    for copy in loads:
        copy.wait()
    swap.wait()

    def state_of(h):
        turned = q[:, columns(h)].astype(jnp.float32).T
        scaled = (turned * lead_row[pl.ds(h, 1), :]).astype(jnp.bfloat16)
        return dot(scaled, g[:, columns(h)], NN)

    def give_step(i, carry):
        for j in range(2):
            given[2 * i + j] = state_of(pair_base + 2 * i + j).astype(given.dtype)
        for j in range(2):
            pair_copy(2 * i + j).start()
        return carry

    def keep_step(i, carry):
        mine[i] = state_of(own_base + i)
        return carry

    lax.fori_loop(0, half_heads // 2, give_step, 0)
    lax.fori_loop(0, half_heads, keep_step, 0, unroll=4)
    fac_copy.wait()

    key_at = lax.broadcasted_iota(jnp.int32, (rows, rows), 0)
    query_at = lax.broadcasted_iota(jnp.int32, (rows, rows), 1)
    allowed[...] = jnp.where(
        (query_at >= key_at) & (doc_of(query_at) == doc_of(key_at)), 1.0, 0.0)
    even = odd == 0

    def inner(h):
        cols = columns(h)
        qh, gh = q[:, cols], g[:, cols]
        along = jnp.broadcast_to(cum[pl.ds(h, 1), :], (rows, rows))
        weight = allowed[...] * jnp.exp(jnp.minimum(along - along.T, 0.0))
        mixed_gv = (weight * dot(v[:, cols], gh, NT)).astype(jnp.bfloat16)
        mixed_qk = (weight * dot(k[:, cols], qh, NT)).astype(jnp.bfloat16)
        key_inner[:, cols] = dot(mixed_gv, qh, NN)
        value_inner[:, cols] = dot(mixed_qk, gh, NN)

    def out_copies(h):
        cols = columns(h)
        return (pltpu.make_async_copy(dk.at[:, cols], dk_hbm.at[:, cols], out_sem.at[0, h]),
                pltpu.make_async_copy(dv.at[:, cols], dv_hbm.at[:, cols], out_sem.at[1, h]))

    def apply(h, state_in):
        cols = columns(h)
        scale = jnp.broadcast_to(tail_row[pl.ds(h, 1), :], (rows, rows)).T
        dk[:, cols] = (key_inner[:, cols] + scale * dot(v[:, cols], state_in, NT)).astype(dk.dtype)
        dv[:, cols] = (value_inner[:, cols] + scale * dot(k[:, cols], state_in, NN)).astype(dv.dtype)

    def chain_step(i, carry):
        h = own_base + i
        pair_copy(i).wait_recv()
        own_state, pair_state = mine[i], other[i].astype(jnp.float32)
        own_factor, pair_factor = factor[pl.ds(h, 1), :], factor_other[pl.ds(h, 1), :]
        state_even = jnp.where(even, own_state, pair_state)
        state_odd = jnp.where(even, pair_state, own_state)
        factor_even = jnp.where(even, own_factor, pair_factor)
        factor_odd = jnp.where(even, pair_factor, own_factor)
        joined = state_even + factor_even * state_odd

        @pl.when(has_after)
        def _():
            chain_copy(i).wait_recv()

        incoming = jnp.where(has_after, later[i].astype(jnp.float32), 0.0)

        @pl.when(has_before)
        def _():
            sent[i] = (joined + (factor_even * factor_odd) * incoming).astype(sent.dtype)
            chain_copy(i).start()

        into_even = (state_odd + factor_odd * incoming).astype(jnp.bfloat16)
        into_odd = incoming.astype(jnp.bfloat16)
        handed[i] = jnp.where(even, into_odd, into_even)
        back_copy(i).start()
        inner(pair_base + i)
        held[i] = jnp.where(even, into_even, into_odd)
        return carry

    def early_step(i, carry):
        inner(own_base + i)
        return carry

    lax.fori_loop(0, half_heads, early_step, 0, unroll=4)
    lax.fori_loop(0, half_heads, chain_step, 0)

    def own_step(i, carry):
        for j in range(2):
            apply(own_base + 2 * i + j, held[2 * i + j])
        for j in range(2):
            for copy in out_copies(own_base + 2 * i + j):
                copy.start()
        return carry

    lax.fori_loop(0, half_heads // 2, own_step, 0)

    def last_step(i, carry):
        back_copy(i).wait_recv()
        apply(pair_base + i, back[i])
        for copy in out_copies(pair_base + i):
            copy.start()
        return carry

    lax.fori_loop(0, half_heads, last_step, 0)

    def drain(i, carry):
        pair_copy(i).wait_send()
        back_copy(i).wait_send()
        for h in (i, half_heads + i):
            for copy in out_copies(h):
                copy.wait()

        @pl.when(has_before)
        def _():
            chain_copy(i).wait_send()

        return carry

    lax.fori_loop(0, half_heads, drain, 0)


def handover(a_in, b_in, a_out, b_out, a_buf, b_buf, in_sem, out_sem):
    pieces = a_buf.shape[0] // 32
    moves = []
    for i in range(pieces):
        part = pl.ds(32 * i, 32)
        for n, (src, buf, dst) in enumerate(((a_in, a_buf, a_out), (b_in, b_buf, b_out))):
            moves.append((pltpu.make_async_copy(src.at[part, :], buf.at[part, :], in_sem.at[n, i]),
                          pltpu.make_async_copy(buf.at[part, :], dst.at[part, :], out_sem.at[n, i])))
    for come, _ in moves:
        come.start()
    for come, go in moves:
        come.wait()
        go.start()
    for _, go in moves:
        go.wait()


def solution(mesh):
    ctx_count = mesh.shape["ctx"]
    wire = jnp.bfloat16 if ctx_count <= 8 else jnp.float32

    def per_device(queries, key_rows, value_rows, out_grad, log_decay, doc_ids):
        rows, features = queries.shape
        heads = log_decay.shape[1]
        anywhere = pl.BlockSpec(memory_space=pl.ANY)
        in_vmem = pl.BlockSpec(memory_space=pltpu.VMEM)
        wide = pltpu.VMEM((rows, features), jnp.bfloat16)
        small = pltpu.VMEM((heads, rows), jnp.float32)
        half = heads // 2
        states = pltpu.VMEM((half, DH, DH), wire)
        kept = pltpu.VMEM((half, DH, DH), jnp.float32)
        rounded = pltpu.VMEM((half, DH, DH), jnp.bfloat16)
        total = pltpu.VMEM((rows, features), jnp.float32)
        square = pltpu.VMEM((rows, rows), jnp.float32)
        many = pltpu.SemaphoreType.DMA((half,))
        shape = jax.ShapeDtypeStruct((rows, features), jnp.bfloat16)
        key_grad, value_grad = pl.pallas_call(
            functools.partial(kernel, ctx_count, heads),
            out_shape=(shape, shape),
            in_specs=[pl.BlockSpec(memory_space=pltpu.SMEM), in_vmem] + [anywhere] * 4,
            out_specs=(anywhere, anywhere),
            scratch_shapes=[wide] * 6 + [small] * 5 + [kept] + [states] * 4 + [rounded] * 3 + [total] * 2 + [square] + [
                pltpu.SemaphoreType.DMA((4,)), pltpu.SemaphoreType.DMA((2,)), pltpu.SemaphoreType.DMA((2,)),
                many, many, many, many, many, many, pltpu.SemaphoreType.DMA((2, heads))],
            compiler_params=pltpu.CompilerParams(
                collective_id=0, has_side_effects=True, vmem_limit_bytes=63 << 20),
        )(doc_ids, log_decay.T, queries, key_rows, value_rows, out_grad)
        pieces = pltpu.SemaphoreType.DMA((2, rows // 32))
        return tuple(pl.pallas_call(
            handover,
            out_shape=(shape, shape),
            in_specs=[anywhere] * 2,
            out_specs=(anywhere, anywhere),
            scratch_shapes=[wide, wide, pieces, pieces],
            compiler_params=pltpu.CompilerParams(vmem_limit_bytes=63 << 20),
        )(key_grad, value_grad))

    placed = (
        P(("group", "ctx"), "tp"),
        P(("group", "ctx"), "tp"),
        P(("group", "ctx"), "tp"),
        P(("group", "ctx", "tp"), None),
        P(("group", "ctx"), "tp"),
        P("group"),
    )
    return jax.shard_map(
        per_device,
        mesh=mesh,
        in_specs=placed,
        out_specs=(P(("group", "ctx"), "tp"), P(("group", "ctx"), "tp")),
        check_vma=False,
    )
```

```python
import functools

import jax
import jax.numpy as jnp
from jax import lax
from jax.experimental import pallas as pl
from jax.experimental.pallas import tpu as pltpu
from jax.sharding import PartitionSpec as P

BLOCK = 64
DH = 128
MESH = pl.DeviceIdType.MESH


def dot(a, b, dims):
    return lax.dot_general(a, b, (dims, ((), ())), preferred_element_type=jnp.float32)


NN = ((1,), (0,))
NT = ((1,), (1,))


def kernel(ctx_count, heads, docs, decay, q_hbm, k_hbm, v_hbm, og_hbm, dk_hbm, dv_hbm,
           dk, dv, q, k, v, g, cum, lead_row, tail_row, factor, factor_other, mine, given, other, sent, later,
           handed, back, held, key_inner, value_inner, allowed,
           load_sem, swap_sem, fac_sem, pair_send, pair_recv, chain_send, chain_recv, back_send, back_recv, out_sem):
    rows = q.shape[0]
    half = og_hbm.shape[0]
    width = q.shape[1]
    group, ctx, tp = lax.axis_index("group"), lax.axis_index("ctx"), lax.axis_index("tp")
    odd = lax.rem(ctx, 2)
    pair = (group, ctx + 1 - 2 * odd, tp)
    core = (group, ctx, 1 - tp)
    before = (group, ctx - 2, tp)
    after = (group, ctx + 2, tp)
    has_before = ctx >= 2
    has_after = ctx < ctx_count - 2

    loads = [pltpu.make_async_copy(src, dst, load_sem.at[i])
             for i, (src, dst) in enumerate(((q_hbm, q), (k_hbm, k), (v_hbm, v)))]
    own_rows = pl.ds(pl.multiple_of(tp * half, half), half)
    loads.append(pltpu.make_async_copy(
        og_hbm.at[:, pl.ds(pl.multiple_of(tp * width, width), width)], g.at[own_rows, :], load_sem.at[3]))
    for copy in loads:
        copy.start()

    barrier = pltpu.get_barrier_semaphore()
    for peer in (pair, core):
        pl.semaphore_signal(barrier, inc=1, device_id=peer, device_id_type=MESH)

    @pl.when(has_before)
    def _():
        pl.semaphore_signal(barrier, inc=1, device_id=before, device_id_type=MESH)

    @pl.when(has_after)
    def _():
        pl.semaphore_signal(barrier, inc=1, device_id=after, device_id_type=MESH)

    pl.semaphore_wait(barrier, 2 + has_before.astype(jnp.int32) + has_after.astype(jnp.int32))

    part = width // 2
    swaps = []
    for n, place in enumerate((1 - odd, odd)):
        theirs = pl.ds(pl.multiple_of((1 - tp) * width + place * part, part), part)
        swaps.append(pltpu.make_async_remote_copy(
            src_ref=og_hbm.at[:, theirs],
            dst_ref=g.at[own_rows, pl.ds(pl.multiple_of(place * part, part), part)],
            send_sem=swap_sem.at[0, n], recv_sem=swap_sem.at[1, n],
            device_id=core, device_id_type=MESH))
    for swap in swaps:
        swap.start()

    blocks = rows // BLOCK
    doc_list = [docs[ctx * blocks + b] for b in range(blocks)]
    first, last = doc_list[0], doc_list[-1]
    prev = docs[jnp.maximum(ctx * blocks - 1, 0)]
    linked = jnp.where((ctx > 0) & (prev == first), 1.0, 0.0).astype(jnp.float32)
    through = jnp.where(first == last, linked, 0.0).astype(jnp.float32)

    def doc_of(position):
        doc = jnp.full(position.shape, first, jnp.int32)
        for b in range(1, blocks):
            doc = jnp.where(position >= b * BLOCK, doc_list[b], doc)
        return doc

    lane = lax.broadcasted_iota(jnp.int32, (heads, rows), 1)
    total = decay[...]
    step = 1
    while step < rows:
        total = total + jnp.where(lane >= step, pltpu.roll(total, step, 1), 0.0)
        step *= 2
    lane_doc = doc_of(lane)
    ending = jnp.broadcast_to(total[:, rows - 1:rows], (heads, rows))
    cum[...] = total
    lead_row[...] = jnp.where(lane_doc == first, jnp.exp(total) * linked, 0.0)
    tail_row[...] = jnp.where(lane_doc == last, jnp.exp(ending - total), 0.0)
    factor[...] = jnp.exp(ending) * through
    fac_copy = pltpu.make_async_remote_copy(
        src_ref=factor, dst_ref=factor_other, send_sem=fac_sem.at[0], recv_sem=fac_sem.at[1],
        device_id=pair, device_id_type=MESH)
    fac_copy.start()

    half_heads = heads // 2
    own_base, pair_base = odd * half_heads, (1 - odd) * half_heads

    def pair_copy(i):
        return pltpu.make_async_remote_copy(
            src_ref=given.at[i], dst_ref=other.at[i], send_sem=pair_send.at[i], recv_sem=pair_recv.at[i],
            device_id=pair, device_id_type=MESH)

    def chain_copy(i):
        return pltpu.make_async_remote_copy(
            src_ref=sent.at[i], dst_ref=later.at[i], send_sem=chain_send.at[i], recv_sem=chain_recv.at[i],
            device_id=before, device_id_type=MESH)

    def back_copy(i):
        return pltpu.make_async_remote_copy(
            src_ref=handed.at[i], dst_ref=back.at[i], send_sem=back_send.at[i], recv_sem=back_recv.at[i],
            device_id=pair, device_id_type=MESH)

    def columns(h):
        return pl.ds(pl.multiple_of(h * DH, DH), DH)

    loads[0].wait()
    loads[3].wait()
    swaps[0].wait()

    def state_of(h):
        turned = q[:, columns(h)].astype(jnp.float32).T
        scaled = (turned * lead_row[pl.ds(h, 1), :]).astype(jnp.bfloat16)
        return dot(scaled, g[:, columns(h)], NN)

    def give_step(i, carry):
        for j in range(2):
            given[2 * i + j] = state_of(pair_base + 2 * i + j).astype(given.dtype)
        for j in range(2):
            pair_copy(2 * i + j).start()
        return carry

    def keep_step(i, carry):
        mine[i] = state_of(own_base + i)
        return carry

    lax.fori_loop(0, half_heads // 2, give_step, 0)
    swaps[1].wait()
    loads[1].wait()
    loads[2].wait()
    lax.fori_loop(0, half_heads, keep_step, 0, unroll=4)
    fac_copy.wait()

    key_at = lax.broadcasted_iota(jnp.int32, (rows, rows), 0)
    query_at = lax.broadcasted_iota(jnp.int32, (rows, rows), 1)
    allowed[...] = jnp.where(
        (query_at >= key_at) & (doc_of(query_at) == doc_of(key_at)), 1.0, 0.0)
    even = odd == 0

    def inner(h):
        cols = columns(h)
        qh, gh = q[:, cols], g[:, cols]
        along = jnp.broadcast_to(cum[pl.ds(h, 1), :], (rows, rows))
        weight = allowed[...] * jnp.exp(jnp.minimum(along - along.T, 0.0))
        mixed_gv = (weight * dot(v[:, cols], gh, NT)).astype(jnp.bfloat16)
        mixed_qk = (weight * dot(k[:, cols], qh, NT)).astype(jnp.bfloat16)
        key_inner[:, cols] = dot(mixed_gv, qh, NN)
        value_inner[:, cols] = dot(mixed_qk, gh, NN)

    def out_copies(h):
        cols = columns(h)
        return (pltpu.make_async_copy(dk.at[:, cols], dk_hbm.at[:, cols], out_sem.at[0, h]),
                pltpu.make_async_copy(dv.at[:, cols], dv_hbm.at[:, cols], out_sem.at[1, h]))

    def apply(h, state_in):
        cols = columns(h)
        scale = jnp.broadcast_to(tail_row[pl.ds(h, 1), :], (rows, rows)).T
        dk[:, cols] = (key_inner[:, cols] + scale * dot(v[:, cols], state_in, NT)).astype(dk.dtype)
        dv[:, cols] = (value_inner[:, cols] + scale * dot(k[:, cols], state_in, NN)).astype(dv.dtype)

    def chain_step(i, carry):
        h = own_base + i
        pair_copy(i).wait_recv()
        own_state, pair_state = mine[i], other[i].astype(jnp.float32)
        own_factor, pair_factor = factor[pl.ds(h, 1), :], factor_other[pl.ds(h, 1), :]
        state_even = jnp.where(even, own_state, pair_state)
        state_odd = jnp.where(even, pair_state, own_state)
        factor_even = jnp.where(even, own_factor, pair_factor)
        factor_odd = jnp.where(even, pair_factor, own_factor)
        joined = state_even + factor_even * state_odd

        @pl.when(has_after)
        def _():
            chain_copy(i).wait_recv()

        incoming = jnp.where(has_after, later[i].astype(jnp.float32), 0.0)

        @pl.when(has_before)
        def _():
            sent[i] = (joined + (factor_even * factor_odd) * incoming).astype(sent.dtype)
            chain_copy(i).start()

        into_even = (state_odd + factor_odd * incoming).astype(jnp.bfloat16)
        into_odd = incoming.astype(jnp.bfloat16)
        handed[i] = jnp.where(even, into_odd, into_even)
        back_copy(i).start()
        inner(pair_base + i)
        held[i] = jnp.where(even, into_even, into_odd)
        return carry

    def early_step(i, carry):
        inner(own_base + i)
        return carry

    lax.fori_loop(0, half_heads, early_step, 0, unroll=4)
    lax.fori_loop(0, half_heads, chain_step, 0)

    def own_step(i, carry):
        for j in range(2):
            apply(own_base + 2 * i + j, held[2 * i + j])
        for j in range(2):
            for copy in out_copies(own_base + 2 * i + j):
                copy.start()
        return carry

    lax.fori_loop(0, half_heads // 2, own_step, 0)

    def last_step(i, carry):
        back_copy(i).wait_recv()
        apply(pair_base + i, back[i])
        for copy in out_copies(pair_base + i):
            copy.start()
        return carry

    lax.fori_loop(0, half_heads, last_step, 0)

    def drain(i, carry):
        pair_copy(i).wait_send()
        back_copy(i).wait_send()
        for h in (i, half_heads + i):
            for copy in out_copies(h):
                copy.wait()

        @pl.when(has_before)
        def _():
            chain_copy(i).wait_send()

        return carry

    lax.fori_loop(0, half_heads, drain, 0)


def handover(a_in, b_in, a_out, b_out, a_buf, b_buf, in_sem, out_sem):
    pieces = a_buf.shape[0] // 32
    moves = []
    for i in range(pieces):
        part = pl.ds(32 * i, 32)
        for n, (src, buf, dst) in enumerate(((a_in, a_buf, a_out), (b_in, b_buf, b_out))):
            moves.append((pltpu.make_async_copy(src.at[part, :], buf.at[part, :], in_sem.at[n, i]),
                          pltpu.make_async_copy(buf.at[part, :], dst.at[part, :], out_sem.at[n, i])))
    for come, _ in moves:
        come.start()
    for come, go in moves:
        come.wait()
        go.start()
    for _, go in moves:
        go.wait()


def solution(mesh):
    ctx_count = mesh.shape["ctx"]
    wire = jnp.bfloat16 if ctx_count <= 8 else jnp.float32

    def per_device(queries, key_rows, value_rows, out_grad, log_decay, doc_ids):
        rows, features = queries.shape
        heads = log_decay.shape[1]
        anywhere = pl.BlockSpec(memory_space=pl.ANY)
        in_vmem = pl.BlockSpec(memory_space=pltpu.VMEM)
        wide = pltpu.VMEM((rows, features), jnp.bfloat16)
        small = pltpu.VMEM((heads, rows), jnp.float32)
        half = heads // 2
        states = pltpu.VMEM((half, DH, DH), wire)
        kept = pltpu.VMEM((half, DH, DH), jnp.float32)
        rounded = pltpu.VMEM((half, DH, DH), jnp.bfloat16)
        total = pltpu.VMEM((rows, features), jnp.float32)
        square = pltpu.VMEM((rows, rows), jnp.float32)
        many = pltpu.SemaphoreType.DMA((half,))
        shape = jax.ShapeDtypeStruct((rows, features), jnp.bfloat16)
        key_grad, value_grad = pl.pallas_call(
            functools.partial(kernel, ctx_count, heads),
            out_shape=(shape, shape),
            in_specs=[pl.BlockSpec(memory_space=pltpu.SMEM), in_vmem] + [anywhere] * 4,
            out_specs=(anywhere, anywhere),
            scratch_shapes=[wide] * 6 + [small] * 5 + [kept] + [states] * 4 + [rounded] * 3 + [total] * 2 + [square] + [
                pltpu.SemaphoreType.DMA((4,)), pltpu.SemaphoreType.DMA((2, 2)), pltpu.SemaphoreType.DMA((2,)),
                many, many, many, many, many, many, pltpu.SemaphoreType.DMA((2, heads))],
            compiler_params=pltpu.CompilerParams(
                collective_id=0, has_side_effects=True, vmem_limit_bytes=63 << 20),
        )(doc_ids, log_decay.T, queries, key_rows, value_rows, out_grad)
        pieces = pltpu.SemaphoreType.DMA((2, rows // 32))
        return tuple(pl.pallas_call(
            handover,
            out_shape=(shape, shape),
            in_specs=[anywhere] * 2,
            out_specs=(anywhere, anywhere),
            scratch_shapes=[wide, wide, pieces, pieces],
            compiler_params=pltpu.CompilerParams(vmem_limit_bytes=63 << 20),
        )(key_grad, value_grad))

    placed = (
        P(("group", "ctx"), "tp"),
        P(("group", "ctx"), "tp"),
        P(("group", "ctx"), "tp"),
        P(("group", "ctx", "tp"), None),
        P(("group", "ctx"), "tp"),
        P("group"),
    )
    return jax.shard_map(
        per_device,
        mesh=mesh,
        in_specs=placed,
        out_specs=(P(("group", "ctx"), "tp"), P(("group", "ctx"), "tp")),
        check_vma=False,
    )
```
